128 devices in a mesh: grp: 2 (over y_lo), row: 16 (over x, z), hid: 4 (over y_hi, core).
Axes of the slice: x: 4, y: 4 (y_hi: 2, y_lo: 2; y = y_hi * 2 + y_lo), z: 4, core: 2. Of those that a mesh axis runs over, the one named last changes fastest.
Arguments:
- token_ids: int32 [512, 64], P(('grp', 'row')), may hold values from 0 to 128255, as said below
- activations: bfloat16 [512, 64, 4096], P(('grp', 'row'), None, 'hid'), may hold values from -6 to 6
- out_grads: bfloat16 [512, 64, 4096], P(('grp', 'row'), None, 'hid'), may hold values from -6 to 6
- proj_in: bfloat16 [64, 4096], P(None, 'hid'), may hold values from -0.09375 to 0.09375
- proj_out: bfloat16 [64, 4096], P(None, 'hid'), may hold values from -0.09375 to 0.09375
- inverse_curvature: float32 [4096, 4096], P('row', ('grp', 'hid')), as said below
- store_grads: bfloat16 [262144, 4096], P(('grp', 'row', 'hid')), may hold values from -1 to 1
- store_order: int32 [262144], P(('grp', 'row', 'hid')), may hold values from 0 to 262143, each once
- example_ids: int32 [512], replicated, may hold values from 0 to 262143
Outputs:
- scores: bfloat16 [262144, 512], P(('grp', 'row', 'hid'))
The draws below stay inside these ranges and needn't reach their ends.
Inputs may be any that keep to these rules, and one draw needn't show every extreme that they name: `token_ids`: 0 marks padding, which only follows a query's tokens; each query has at least 16 tokens that are not padding. `example_ids`: each query's id names a stored example. `inverse_curvature`: symmetric.
All inputs are finite; a program needn't handle non-finite values.
Results may differ from the reference program's by a relative error of at most 0.013.
Values may be sent and summed in bfloat16 or wider, within the bound.
No kernel may reach another device: no remote copies, remote signals or barrier semaphores. Data moves between devices by JAX's collectives and lax.ppermute only.
A program may use at most 128 MiB of HBM per device.

```python
import jax
import jax.numpy as jnp
from jax import lax

D = 4096
VOCAB = 128256
PROJ = 64
QLEN = 64
STORE_DEV = 2048
K = 4096
QUERIES = 512
ROWS = 262144


def draw_token_ids(key, part):
    key_len = jax.random.fold_in(key, 11)
    key_ids = jax.random.fold_in(key, 12)
    lengths = jax.random.randint(key_len, (QUERIES,), QLEN // 4, QLEN + 1)
    tokens = jax.random.randint(key_ids, (QUERIES, QLEN), 1, VOCAB)
    positions = jnp.arange(QLEN)[None, :]
    return jnp.where(positions < lengths[:, None], tokens, 0).astype(jnp.int32)


def draw_inverse_curvature(key, part):
    key_diag = jax.random.fold_in(key, 21)
    key_off = jax.random.fold_in(key, 22)
    diagonal = jnp.exp(jax.random.uniform(key_diag, (K,), jnp.float32, 0.0, jnp.log(4.0)))
    spread = 0.6
    noise = jax.random.normal(key_off, (K, K), jnp.float32) * (spread / K ** 0.5)
    symmetric = (noise + noise.T) * 0.5 ** 0.5
    eye = jnp.eye(K, dtype=jnp.float32)
    return (symmetric * (1.0 - eye) + eye * diagonal[None, :]).astype(jnp.float32)


def plant(array, rng, smallest, high):
    dims = array.shape
    index_at = [jax.random.randint(jax.random.fold_in(rng, axis), (), 0, dims[axis]) for axis in range(len(dims))]
    array = array.at[tuple(index_at)].set(smallest)
    longest = dims.index(max(dims))
    index_at[longest] = (index_at[longest] + 1) % dims[longest]
    return array.at[tuple(index_at)].set(high)


def level_of(own_key, shape, shards, least, top_value):
    loudness = 1.0
    for position, parts in shards:
        heights = jax.random.uniform(jax.random.fold_in(jax.random.fold_in(own_key, 6), position), (parts,), jnp.float32, least / len(shards), top_value / len(shards))
        loudness = loudness * jnp.repeat(jnp.exp(heights), shape[position] // parts).reshape((-1,) + (1,) * (len(shape) - 1 - position))
    return loudness


def scatter_about(rng, dims, scale, reach, pieces=(), kind=jnp.bfloat16):
    level = level_of(rng, dims, pieces, -0.22, 0.18) if pieces else 1.0
    entries = jax.random.normal(rng, dims, jnp.float32) * scale * level
    return jnp.minimum(jnp.maximum(entries, -reach), reach).astype(kind)


def setup_inputs(seed: int = 0) -> dict:
    seeds = jax.random.split(jax.random.key(seed), 10)
    return {
        "token_ids": draw_token_ids(jax.random.fold_in(seeds[9], 71), 0),
        "activations": scatter_about(seeds[1], (QUERIES, QLEN, D), 1.0, 6.0, ((0, 32), (2, 4))),
        "out_grads": scatter_about(seeds[2], (QUERIES, QLEN, D), 1.0, 6.0, ((0, 32), (2, 4))),
        "proj_in": scatter_about(seeds[3], (PROJ, D), D ** -0.5, 0.09375, ((1, 4),)),
        "proj_out": scatter_about(seeds[4], (PROJ, D), D ** -0.5, 0.09375, ((1, 4),)),
        "inverse_curvature": draw_inverse_curvature(jax.random.fold_in(seeds[9], 71), 0),
        "store_grads": scatter_about(seeds[6], (ROWS, K), 0.125, 1.0, ((0, 128),)),
        "store_order": jax.random.permutation(seeds[7], ROWS).astype(jnp.int32),
        "example_ids": plant(jax.random.randint(seeds[8], (QUERIES,), 0, ROWS), jax.random.fold_in(seeds[8], 1), 0, ROWS - 1).astype(jnp.int32),
    }


def reference(token_ids, activations, out_grads, proj_in, proj_out, inverse_curvature, store_grads, store_order, example_ids):
    usable = (token_ids > 0).astype(jnp.float32)
    counted = jnp.sum(usable, axis=1, keepdims=True)
    weights = usable / counted
    flat_inputs = activations.reshape(QUERIES * QLEN, D)
    flat_grads = out_grads.reshape(QUERIES * QLEN, D)
    in_side = jnp.dot(flat_inputs, proj_in.T, preferred_element_type=jnp.float32).reshape(QUERIES, QLEN, PROJ)
    out_side = jnp.dot(flat_grads, proj_out.T, preferred_element_type=jnp.float32).reshape(QUERIES, QLEN, PROJ)
    scaled = out_side * weights[:, :, None]
    query_grads = jnp.einsum("qla,qlb->qab", scaled, in_side).reshape(QUERIES, PROJ * PROJ)
    preconditioned = jnp.dot(query_grads, inverse_curvature, precision=lax.Precision.HIGHEST, preferred_element_type=jnp.float32).astype(jnp.bfloat16)
    blocks = ROWS // STORE_DEV
    grads_blocked = store_grads.reshape(blocks, STORE_DEV, PROJ * PROJ)
    order_blocked = store_order.reshape(blocks, STORE_DEV)

    def score_block(pair):
        stored, order_part = pair
        raw = jnp.dot(stored, preconditioned.T, preferred_element_type=jnp.float32)
        is_self = order_part[:, None] == example_ids[None, :]
        return jnp.where(is_self, 0.0, raw).astype(jnp.bfloat16)

    scores = lax.map(score_block, (grads_blocked, order_blocked))
    return scores.reshape(ROWS, QUERIES)
```

```python
import functools

import jax
import jax.numpy as jnp
from jax import lax
from jax.experimental import pallas as pl
from jax.experimental.pallas import tpu as pltpu
from jax.sharding import PartitionSpec as P

AXES = ("grp", "row", "hid")
NT = (((1,), (1,)), ((), ()))
TN = (((0,), (0,)), ((), ()))
F32 = jnp.float32
BF16 = jnp.bfloat16


def linear(y, row, core):
    return (y % 2) * 64 + row * 4 + (y // 2) * 2 + core


def moved(value, dy, dcore):
    pairs = [
        (linear(y, row, core), linear((y + dy) % 4, row, core ^ dcore))
        for y in range(4)
        for row in range(16)
        for core in range(2)
    ]
    return lax.ppermute(value, AXES, pairs)


def project_kernel(which, grads, inputs, w_out, w_in, out):
    out[0, :, :64] = lax.dot_general(grads[...], w_out[...], NT, preferred_element_type=F32).astype(BF16)
    out[0, :, 64:] = lax.dot_general(inputs[...], w_in[...], NT, preferred_element_type=F32).astype(BF16)


def project(which, grads, inputs, w_out, w_in):
    tokens, width = 256, grads.shape[1]
    rows = pl.BlockSpec((tokens, width), lambda i, which: (2 * i + which[0], 0))
    whole = pl.BlockSpec((64, width), lambda i, which: (0, 0))
    return pl.pallas_call(
        project_kernel,
        out_shape=jax.ShapeDtypeStruct((2, tokens, 128), BF16),
        grid_spec=pltpu.PrefetchScalarGridSpec(
            num_scalar_prefetch=1,
            grid=(2,),
            in_specs=[rows, rows, whole, whole],
            out_specs=pl.BlockSpec((1, tokens, 128), lambda i, which: (i, 0, 0)),
        ),
        cost_estimate=pl.CostEstimate(
            flops=4 * tokens * width * 128, bytes_accessed=4 * tokens * width * 2, transcendentals=0
        ),
        compiler_params=pltpu.CompilerParams(vmem_limit_bytes=16 << 20),
        name="project",
    )(which, grads, inputs, w_out, w_in)


def join_kernel(where, kept, came, send, mine):
    yh = where[0]
    send[...] = (kept[1 - yh].astype(F32) + came[1 - yh].astype(F32)).astype(BF16)
    mine[...] = kept[yh].astype(F32) + came[yh].astype(F32)


def join(where, kept, came):
    return pl.pallas_call(
        join_kernel,
        out_shape=(jax.ShapeDtypeStruct((256, 128), BF16), jax.ShapeDtypeStruct((256, 128), F32)),
        in_specs=[pl.BlockSpec(memory_space=pltpu.SMEM)] + [pl.BlockSpec(memory_space=pltpu.VMEM)] * 2,
        out_specs=[pl.BlockSpec(memory_space=pltpu.VMEM)] * 2,
        compiler_params=pltpu.CompilerParams(vmem_limit_bytes=8 << 20),
        name="join",
    )(where, kept, came)


def outer_kernel(where, ids, mine, came, out, held):
    usable = (ids[...] > 0).astype(F32)
    for q in range(4):
        count = jnp.sum(usable[q : q + 1], axis=1, keepdims=True)
        both = mine[64 * q : 64 * (q + 1)] + came[64 * q : 64 * (q + 1)].astype(F32)
        position = lax.broadcasted_iota(jnp.int32, (64, 128), 0).astype(F32)
        both = jnp.where(position < count, both, 0.0).astype(BF16)
        held[...] = lax.dot_general(both[:, :64], both[:, 64:], TN, preferred_element_type=F32) / count
        even, odd = held[pl.ds(0, 32, 2), :], held[pl.ds(1, 32, 2), :]
        out[q] = jnp.concatenate([even, odd], axis=1).astype(BF16)


def outer(ids, mine, came):
    return pl.pallas_call(
        functools.partial(outer_kernel, None),
        out_shape=jax.ShapeDtypeStruct((4, 32, 128), BF16),
        in_specs=[pl.BlockSpec(memory_space=pltpu.VMEM)] * 3,
        out_specs=pl.BlockSpec(memory_space=pltpu.VMEM),
        scratch_shapes=[pltpu.VMEM((64, 64), F32)],
        compiler_params=pltpu.CompilerParams(vmem_limit_bytes=8 << 20),
        name="outer",
    )(ids, mine, came)


def precondition_kernel(where, grads, *refs):
    blocks, (keep, send) = refs[:8], refs[8:]
    total = jnp.zeros((64, 256), F32)
    for i, block in enumerate(blocks):
        start = pl.multiple_of(where[1 + i] * 512, 512)
        total += lax.dot_general(grads[:, pl.ds(start, 512)], block[...], NT, preferred_element_type=F32)
    low, high = total[:, :128].astype(BF16), total[:, 128:].astype(BF16)

    @pl.when(where[0] == 0)
    def _():
        keep[...], send[...] = low, high

    @pl.when(where[0] != 0)
    def _():
        keep[...], send[...] = high, low


def precondition(where, grads, blocks):
    return pl.pallas_call(
        precondition_kernel,
        out_shape=(jax.ShapeDtypeStruct((64, 128), BF16),) * 2,
        in_specs=[pl.BlockSpec(memory_space=pltpu.SMEM)] + [pl.BlockSpec(memory_space=pltpu.VMEM)] * 9,
        out_specs=[pl.BlockSpec(memory_space=pltpu.VMEM)] * 2,
        compiler_params=pltpu.CompilerParams(vmem_limit_bytes=16 << 20),
        name="precondition",
    )(where, grads, *blocks)


def load_queries(raw, held, sem):
    copies = []
    for s in range(64):
        g, rk, yh = s // 32, s % 32 // 2, s % 2
        copies.append(
            pltpu.make_async_copy(raw.at[s], held.at[g, :, yh, :, rk * 128 : (rk + 1) * 128], sem.at[s])
        )
    for copy in copies:
        copy.start()
    for copy in copies:
        copy.wait()


def first_kernel(which, *refs):
    stores, raw, out, held, sem = refs[:16], *refs[16:]

    @pl.when(pl.program_id(0) == 0)
    def _():
        load_queries(raw, held, sem)

    rows = jnp.concatenate([s[...] for s in stores], axis=1)
    queries = held.reshape(512, 2048)[...]
    out[...] = lax.dot_general(rows, queries, NT, preferred_element_type=F32)


def second_kernel(which, *refs):
    stores, raw, before, order, ids, out, held, sem = refs[:16], *refs[16:]

    @pl.when(pl.program_id(0) == 0)
    def _():
        load_queries(raw, held, sem)

    rows = jnp.concatenate([s[...] for s in stores], axis=1)
    queries = held.reshape(512, 2048)[...]
    total = before[...] + lax.dot_general(rows, queries, NT, preferred_element_type=F32)
    out[...] = jnp.where(order[...] == ids[...], 0.0, total).astype(BF16)


def product(kernel, which, store, raw, extra, extra_specs, out_dtype, name):
    tile, depth = 512, store.shape[0]
    stores = [
        pl.BlockSpec((tile, 128), functools.partial(lambda rk, i, which: (i, 2 * rk + which[0]), rk))
        for rk in range(16)
    ]
    return pl.pallas_call(
        kernel,
        out_shape=jax.ShapeDtypeStruct((depth, 512), out_dtype),
        grid_spec=pltpu.PrefetchScalarGridSpec(
            num_scalar_prefetch=1,
            grid=(depth // tile,),
            in_specs=[*stores, pl.BlockSpec(memory_space=pl.ANY), *extra_specs],
            out_specs=pl.BlockSpec((tile, 512), lambda i, which: (i, 0)),
            scratch_shapes=[pltpu.VMEM((2, 16, 2, 8, 2048), BF16), pltpu.SemaphoreType.DMA((64,))],
        ),
        cost_estimate=pl.CostEstimate(
            flops=2 * depth * 512 * 2048, bytes_accessed=depth * 2048 * 2 + depth * 512 * 4, transcendentals=0
        ),
        compiler_params=pltpu.CompilerParams(vmem_limit_bytes=32 << 20),
        name=name,
    )(which, *[store] * 16, raw, *extra)


def local(
    token_ids,
    activations,
    out_grads,
    proj_in,
    proj_out,
    inverse_curvature,
    store_grads,
    store_order,
    example_ids,
):
    width = activations.shape[2]
    hid = lax.axis_index("hid")
    grp = lax.axis_index("grp")
    core, yh = hid % 2, hid // 2
    y = yh * 2 + grp

    own = inverse_curvature.astype(BF16)
    blocks = [own] + [moved(own, dy, 0) for dy in (1, 3, 2)]
    from_y = [y, (y + 3) % 4, (y + 1) % 4, (y + 2) % 4]

    flat_inputs = activations.reshape(-1, width)
    flat_grads = out_grads.reshape(-1, width)
    away = project(jnp.stack([1 - core]), flat_grads, flat_inputs, proj_out, proj_in)
    came = moved(away, 0, 1)
    kept = project(jnp.stack([core]), flat_grads, flat_inputs, proj_out, proj_in)
    send, mine = join(jnp.stack([yh]), kept, came)
    came = moved(send, 2, 0)
    ids = lax.dynamic_slice_in_dim(token_ids, hid * 4, 4, 0)
    grads = outer(ids, mine, came)

    grads = lax.all_to_all(jnp.broadcast_to(grads[None], (16, 4, 32, 128)), "row", 0, 0, tiled=True)
    grads = grads.reshape(64, 4096)

    theirs = moved(jnp.stack(blocks), 0, 1)
    blocks = blocks + [theirs[i] for i in range(4)]
    places = [(v % 2) * 4 + (v // 2) * 2 + core for v in from_y]
    places += [(v % 2) * 4 + (v // 2) * 2 + 1 - core for v in from_y]
    keep, send = precondition(jnp.stack([core, *places]), grads, blocks)
    came = moved(send, 0, 1)
    keep, came = keep.reshape(16, 1, 4, 128), came.reshape(16, 1, 4, 128)
    mine = jnp.where(
        core == 0, jnp.concatenate([keep, came], axis=1), jnp.concatenate([came, keep], axis=1)
    ).reshape(16, 8, 128)
    groups = [
        [linear(yl + 2 * yu, row, c) for yl in range(2) for row in range(16) for yu in range(2)] for c in range(2)
    ]
    near = lax.all_to_all(
        jnp.broadcast_to(mine[None], (64, 16, 8, 128)), AXES, 0, 0, axis_index_groups=groups, tiled=True
    )
    far = moved(near, 0, 1)
    part = product(first_kernel, jnp.stack([core]), store_grads, near, [], [], F32, "first")
    return product(
        second_kernel,
        jnp.stack([1 - core]),
        store_grads,
        far,
        [part, store_order[:, None], example_ids[None, :]],
        [
            pl.BlockSpec((512, 512), lambda i, which: (i, 0)),
            pl.BlockSpec((512, 1), lambda i, which: (i, 0)),
            pl.BlockSpec((1, 512), lambda i, which: (0, 0)),
        ],
        BF16,
        "second",
    )


def solution(mesh):
    placed = (
        P(("grp", "row"), None),
        P(("grp", "row"), None, "hid"),
        P(("grp", "row"), None, "hid"),
        P(None, "hid"),
        P(None, "hid"),
        P("row", ("grp", "hid")),
        P(("grp", "row", "hid"), None),
        P(("grp", "row", "hid")),
        P(),
    )
    return jax.shard_map(
        local, mesh=mesh, in_specs=placed, out_specs=P(("grp", "row", "hid"), None), check_vma=False
    )
```

```python
import functools

import jax
import jax.numpy as jnp
from jax import lax
from jax.experimental import pallas as pl
from jax.experimental.pallas import tpu as pltpu
from jax.sharding import PartitionSpec as P

AXES = ("grp", "row", "hid")
NT = (((1,), (1,)), ((), ()))
TN = (((0,), (0,)), ((), ()))
F32 = jnp.float32
BF16 = jnp.bfloat16


def linear(y, row, core):
    return (y % 2) * 64 + row * 4 + (y // 2) * 2 + core


def copied(value, groups):
    count = len(groups[0])
    return lax.all_to_all(
        jnp.broadcast_to(value[None], (count, *value.shape)), AXES, 0, 0, axis_index_groups=groups, tiled=True
    )


def groups_of(key):
    found = {}
    for device in sorted(
        (linear(y, x * 4 + z, core), key(x, y, z, core))
        for x in range(4)
        for y in range(4)
        for z in range(4)
        for core in range(2)
    ):
        found.setdefault(device[1], []).append(device[0])
    return list(found.values())


def moved(value, dy, dcore):
    pairs = [
        (linear(y, row, core), linear((y + dy) % 4, row, core ^ dcore))
        for y in range(4)
        for row in range(16)
        for core in range(2)
    ]
    return lax.ppermute(value, AXES, pairs)


def project_kernel(which, grads, inputs, w_out, w_in, out):
    out[0, :, :64] = lax.dot_general(grads[...], w_out[...], NT, preferred_element_type=F32).astype(BF16)
    out[0, :, 64:] = lax.dot_general(inputs[...], w_in[...], NT, preferred_element_type=F32).astype(BF16)


def project(which, grads, inputs, w_out, w_in):
    tokens, width = 256, grads.shape[1]
    rows = pl.BlockSpec((tokens, width), lambda i, which: (2 * i + which[0], 0))
    whole = pl.BlockSpec((64, width), lambda i, which: (0, 0))
    return pl.pallas_call(
        project_kernel,
        out_shape=jax.ShapeDtypeStruct((2, tokens, 128), BF16),
        grid_spec=pltpu.PrefetchScalarGridSpec(
            num_scalar_prefetch=1,
            grid=(2,),
            in_specs=[rows, rows, whole, whole],
            out_specs=pl.BlockSpec((1, tokens, 128), lambda i, which: (i, 0, 0)),
        ),
        cost_estimate=pl.CostEstimate(
            flops=4 * tokens * width * 128, bytes_accessed=4 * tokens * width * 2, transcendentals=0
        ),
        compiler_params=pltpu.CompilerParams(vmem_limit_bytes=16 << 20),
        name="project",
    )(which, grads, inputs, w_out, w_in)


def join_kernel(where, kept, came, send, mine):
    yh = where[0]
    send[...] = (kept[1 - yh].astype(F32) + came[1 - yh].astype(F32)).astype(BF16)
    mine[...] = kept[yh].astype(F32) + came[yh].astype(F32)


def join(where, kept, came):
    return pl.pallas_call(
        join_kernel,
        out_shape=(jax.ShapeDtypeStruct((256, 128), BF16), jax.ShapeDtypeStruct((256, 128), F32)),
        in_specs=[pl.BlockSpec(memory_space=pltpu.SMEM)] + [pl.BlockSpec(memory_space=pltpu.VMEM)] * 2,
        out_specs=[pl.BlockSpec(memory_space=pltpu.VMEM)] * 2,
        compiler_params=pltpu.CompilerParams(vmem_limit_bytes=8 << 20),
        name="join",
    )(where, kept, came)


def outer_kernel(where, ids, mine, came, out, held):
    usable = (ids[...] > 0).astype(F32)
    for q in range(4):
        count = jnp.sum(usable[q : q + 1], axis=1, keepdims=True)
        both = mine[64 * q : 64 * (q + 1)] + came[64 * q : 64 * (q + 1)].astype(F32)
        position = lax.broadcasted_iota(jnp.int32, (64, 128), 0).astype(F32)
        both = jnp.where(position < count, both, 0.0).astype(BF16)
        held[...] = lax.dot_general(both[:, :64], both[:, 64:], TN, preferred_element_type=F32) / count
        even, odd = held[pl.ds(0, 32, 2), :], held[pl.ds(1, 32, 2), :]
        out[q] = jnp.concatenate([even, odd], axis=1).astype(BF16)


def outer(ids, mine, came):
    return pl.pallas_call(
        functools.partial(outer_kernel, None),
        out_shape=jax.ShapeDtypeStruct((4, 32, 128), BF16),
        in_specs=[pl.BlockSpec(memory_space=pltpu.VMEM)] * 3,
        out_specs=pl.BlockSpec(memory_space=pltpu.VMEM),
        scratch_shapes=[pltpu.VMEM((64, 64), F32)],
        compiler_params=pltpu.CompilerParams(vmem_limit_bytes=8 << 20),
        name="outer",
    )(ids, mine, came)


def precondition_kernel(core, grads, near, far, keep, send):
    total = jnp.zeros((64, 256), F32)
    for blocks, side in ((near, core[0]), (far, 1 - core[0])):
        for i in range(4):
            start = pl.multiple_of((2 * i + side) * 512, 512)
            total += lax.dot_general(grads[:, pl.ds(start, 512)], blocks[i], NT, preferred_element_type=F32)
    low, high = total[:, :128].astype(BF16), total[:, 128:].astype(BF16)

    @pl.when(core[0] == 0)
    def _():
        keep[...], send[...] = low, high

    @pl.when(core[0] != 0)
    def _():
        keep[...], send[...] = high, low


def precondition(core, grads, near, far):
    return pl.pallas_call(
        precondition_kernel,
        out_shape=(jax.ShapeDtypeStruct((64, 128), BF16),) * 2,
        in_specs=[pl.BlockSpec(memory_space=pltpu.SMEM)] + [pl.BlockSpec(memory_space=pltpu.VMEM)] * 3,
        out_specs=[pl.BlockSpec(memory_space=pltpu.VMEM)] * 2,
        compiler_params=pltpu.CompilerParams(vmem_limit_bytes=16 << 20),
        name="precondition",
    )(core, grads, near, far)


def load_queries(raw, held, sem):
    copies = []
    for s in range(64):
        line, g, plane, yh = s // 16, s % 16 // 8, s % 8 // 2, s % 2
        slot = line * 4 + plane
        copies.append(
            pltpu.make_async_copy(raw.at[s], held.at[g, :, yh, :, slot * 128 : (slot + 1) * 128], sem.at[s])
        )
    for copy in copies:
        copy.start()
    for copy in copies:
        copy.wait()


def first_kernel(which, *refs):
    stores, raw, out, held, sem = refs[:16], *refs[16:]

    @pl.when(pl.program_id(0) == 0)
    def _():
        load_queries(raw, held, sem)

    rows = jnp.concatenate([s[...] for s in stores], axis=1)
    queries = held.reshape(512, 2048)[...]
    out[...] = lax.dot_general(rows, queries, NT, preferred_element_type=F32)


def second_kernel(which, *refs):
    stores, raw, before, order, ids, out, held, sem = refs[:16], *refs[16:]

    @pl.when(pl.program_id(0) == 0)
    def _():
        load_queries(raw, held, sem)

    rows = jnp.concatenate([s[...] for s in stores], axis=1)
    queries = held.reshape(512, 2048)[...]
    total = before[...] + lax.dot_general(rows, queries, NT, preferred_element_type=F32)
    out[...] = jnp.where(order[...] == ids[...], 0.0, total).astype(BF16)


def product(kernel, which, store, raw, extra, extra_specs, out_dtype, name):
    tile, depth = 512, store.shape[0]
    stores = [
        pl.BlockSpec((tile, 128), functools.partial(lambda slot, i, which: (i, which[slot]), slot))
        for slot in range(16)
    ]
    return pl.pallas_call(
        kernel,
        out_shape=jax.ShapeDtypeStruct((depth, 512), out_dtype),
        grid_spec=pltpu.PrefetchScalarGridSpec(
            num_scalar_prefetch=1,
            grid=(depth // tile,),
            in_specs=[*stores, pl.BlockSpec(memory_space=pl.ANY), *extra_specs],
            out_specs=pl.BlockSpec((tile, 512), lambda i, which: (i, 0)),
            scratch_shapes=[pltpu.VMEM((2, 16, 2, 8, 2048), BF16), pltpu.SemaphoreType.DMA((64,))],
        ),
        cost_estimate=pl.CostEstimate(
            flops=2 * depth * 512 * 2048, bytes_accessed=depth * 2048 * 2 + depth * 512 * 4, transcendentals=0
        ),
        compiler_params=pltpu.CompilerParams(vmem_limit_bytes=32 << 20),
        name=name,
    )(which, *[store] * 16, raw, *extra)


def local(
    token_ids,
    activations,
    out_grads,
    proj_in,
    proj_out,
    inverse_curvature,
    store_grads,
    store_order,
    example_ids,
):
    width = activations.shape[2]
    hid = lax.axis_index("hid")
    core, yh = hid & 1, hid >> 1

    lines = groups_of(lambda x, y, z, core: (x, z, core))
    near = copied(inverse_curvature.astype(BF16), lines)

    flat_inputs = activations.reshape(-1, width)
    flat_grads = out_grads.reshape(-1, width)
    away = project(jnp.stack([1 - core]), flat_grads, flat_inputs, proj_out, proj_in)
    came = moved(away, 0, 1)
    kept = project(jnp.stack([core]), flat_grads, flat_inputs, proj_out, proj_in)
    send, mine = join(jnp.stack([yh]), kept, came)
    came = moved(send, 2, 0)
    ids = lax.dynamic_slice_in_dim(token_ids, hid * 4, 4, 0)
    grads = outer(ids, mine, came)

    grads, near = lax.optimization_barrier((grads, near))
    far = moved(near, 0, 1)
    grads = lax.all_to_all(jnp.broadcast_to(grads[None], (16, 4, 32, 128)), "row", 0, 0, tiled=True)
    keep, send = precondition(jnp.stack([core]), grads.reshape(64, 4096), near, far)
    came = moved(send, 0, 1)
    keep, came = keep.reshape(16, 1, 4, 128), came.reshape(16, 1, 4, 128)
    mine = jnp.where(
        core == 0, jnp.concatenate([keep, came], axis=1), jnp.concatenate([came, keep], axis=1)
    ).reshape(16, 8, 128)
    planes = groups_of(lambda x, y, z, core: (core, z if core else x))
    lines = groups_of(lambda x, y, z, core: (core, y, x if core else z))
    near = copied(copied(mine, planes), lines).reshape(64, 16, 8, 128)
    far = moved(near, 0, 1)
    slots = jnp.arange(16, dtype=jnp.int32)
    turned = slots % 4 * 4 + slots // 4
    near_columns = jnp.where(core == 0, 2 * slots, 2 * turned + 1)
    far_columns = jnp.where(core == 0, 2 * turned + 1, 2 * slots)
    part = product(first_kernel, near_columns, store_grads, near, [], [], F32, "first")
    return product(
        second_kernel,
        far_columns,
        store_grads,
        far,
        [part, store_order[:, None], example_ids[None, :]],
        [
            pl.BlockSpec((512, 512), lambda i, which: (i, 0)),
            pl.BlockSpec((512, 1), lambda i, which: (i, 0)),
            pl.BlockSpec((1, 512), lambda i, which: (0, 0)),
        ],
        BF16,
        "second",
    )


def solution(mesh):
    placed = (
        P(("grp", "row"), None),
        P(("grp", "row"), None, "hid"),
        P(("grp", "row"), None, "hid"),
        P(None, "hid"),
        P(None, "hid"),
        P("row", ("grp", "hid")),
        P(("grp", "row", "hid"), None),
        P(("grp", "row", "hid")),
        P(),
    )
    return jax.shard_map(
        local, mesh=mesh, in_specs=placed, out_specs=P(("grp", "row", "hid"), None), check_vma=False
    )
```

```python
import functools

import jax
import jax.numpy as jnp
from jax import lax
from jax.experimental import pallas as pl
from jax.experimental.pallas import tpu as pltpu
from jax.sharding import PartitionSpec as P

AXES = ("grp", "row", "hid")
NT = (((1,), (1,)), ((), ()))
TN = (((0,), (0,)), ((), ()))
F32 = jnp.float32
BF16 = jnp.bfloat16
VMEM = pl.BlockSpec(memory_space=pltpu.VMEM)
HBM = pl.BlockSpec(memory_space=pltpu.HBM)
TILE = 512
STEPS = (1, 3, 2)


def linear(x, y, z, core):
    return (y % 2) * 64 + (x * 4 + z) * 4 + (y // 2) * 2 + core


def everywhere():
    return [(x, y, z, core) for x in range(4) for y in range(4) for z in range(4) for core in range(2)]


def moved(value, target):
    pairs = [(linear(*place), linear(*target(*place))) for place in everywhere()]
    return lax.ppermute(value, AXES, pairs)


def across(value):
    return moved(value, lambda x, y, z, core: (x, y, z, 1 - core))


def along_y(value, step):
    return moved(value, lambda x, y, z, core: (x, (y + step) % 4, z, core))


def along_line(value, step):
    return moved(
        value,
        lambda x, y, z, core: (x, y, (z + step) % 4, 1) if core else ((x + step) % 4, y, z, 0),
    )


def copied(value, key):
    found = {}
    for place in sorted(everywhere(), key=lambda place: linear(*place)):
        found.setdefault(key(*place), []).append(linear(*place))
    groups = list(found.values())
    count = len(groups[0])
    return lax.all_to_all(
        jnp.broadcast_to(value[None], (count, *value.shape)), AXES, 0, 0, axis_index_groups=groups, tiled=True
    )


def in_hbm(value):
    return pltpu.with_memory_space_constraint(value, pltpu.HBM)


def core_and_half():
    hid = lax.axis_index("hid")
    return hid & 1, hid >> 1


def packed(inside, outside):
    return (
        jnp.concatenate([inside[:256], inside[256:]], axis=1),
        jnp.concatenate([outside[128 * i : 128 * (i + 1)] for i in range(4)], axis=1),
    )


def project_kernel(away, grads, inputs, w_out, w_in, send, keep, grads_in, inputs_in, w_sorted, sem, w_sem):
    core, half = core_and_half()
    start = (1 - half if away else half) * 512
    weights, tiles = [], []
    for side in range(2):
        for part in range(4):
            rows = pl.ds(pl.multiple_of((2 * part + (core ^ side)) * 8, 8), 8)
            weights.append(
                pltpu.make_async_copy(
                    w_out.at[rows, :], w_sorted.at[pl.ds(side * 32 + part * 8, 8), :], w_sem.at[side * 4 + part]
                )
            )
    for i in range(2):
        rows = pl.ds(pl.multiple_of(start + i * 256, 256), 256)
        tiles.append(pltpu.make_async_copy(grads.at[rows, :], grads_in.at[i], sem.at[2 * i]))
        tiles.append(pltpu.make_async_copy(inputs.at[rows, :], inputs_in.at[i], sem.at[2 * i + 1]))
    for copy in weights + tiles:
        copy.start()
    for copy in weights:
        copy.wait()
    outside, inside = [], []
    for i in range(2):
        tiles[2 * i].wait()
        outside.append(lax.dot_general(grads_in[i], w_sorted[...], NT, preferred_element_type=F32))
        tiles[2 * i + 1].wait()
        inside.append(lax.dot_general(inputs_in[i], w_in[...], NT, preferred_element_type=F32))
    outside, inside = jnp.concatenate(outside, axis=0), jnp.concatenate(inside, axis=0)
    keep[:256], keep[256:] = packed(inside, outside[:, :32])
    for rows, value in zip((slice(0, 256), slice(256, 384)), packed(inside, outside[:, 32:])):
        send[rows] = value.astype(BF16)


def project(away, grads, inputs, w_out, w_in):
    width = grads.shape[1]
    return pl.pallas_call(
        functools.partial(project_kernel, away),
        out_shape=(jax.ShapeDtypeStruct((384, 128), BF16), jax.ShapeDtypeStruct((384, 128), F32)),
        in_specs=[HBM, HBM, HBM, VMEM],
        out_specs=(VMEM, VMEM),
        scratch_shapes=[
            pltpu.VMEM((2, 256, width), BF16),
            pltpu.VMEM((2, 256, width), BF16),
            pltpu.VMEM((64, width), BF16),
            pltpu.SemaphoreType.DMA((4,)),
            pltpu.SemaphoreType.DMA((8,)),
        ],
        cost_estimate=pl.CostEstimate(
            flops=2 * 512 * width * 128, bytes_accessed=2 * 512 * width * 2, transcendentals=0
        ),
        compiler_params=pltpu.CompilerParams(vmem_limit_bytes=8 << 20),
        name="project_away" if away else "project_kept",
    )(in_hbm(grads), in_hbm(inputs), in_hbm(w_out), w_in)


def outer_kernel(ids, kept, came_core, came_half, out, held):
    _, half = core_and_half()
    usable = (ids[pl.ds(pl.multiple_of(half * 8, 8), 8), :] > 0).astype(F32)
    counts = jnp.sum(usable, axis=1, keepdims=True)
    total = kept[...] + came_core[...].astype(F32) + came_half[...].astype(F32)
    position = lax.broadcasted_iota(jnp.int32, (64, 32), 0).astype(F32)
    for q in range(8):
        count = counts[q : q + 1]
        inside = total[64 * (q % 4) : 64 * (q % 4 + 1), 64 * (q // 4) : 64 * (q // 4 + 1)]
        outside = total[256 + 64 * (q % 2) : 320 + 64 * (q % 2), 32 * (q // 2) : 32 * (q // 2 + 1)]
        outside = jnp.where(position < count, outside, 0.0)
        held[q] = (
            lax.dot_general(outside.astype(BF16), inside.astype(BF16), TN, preferred_element_type=F32) / count
        )
        even, odd = held[q, pl.ds(0, 16, 2), :], held[q, pl.ds(1, 16, 2), :]
        out[q] = jnp.concatenate([even, odd], axis=1).astype(BF16)


def outer(ids, kept, came_core, came_half):
    return pl.pallas_call(
        outer_kernel,
        out_shape=jax.ShapeDtypeStruct((8, 16, 128), BF16),
        in_specs=[VMEM] * 4,
        out_specs=VMEM,
        scratch_shapes=[pltpu.VMEM((8, 32, 64), F32)],
        compiler_params=pltpu.CompilerParams(vmem_limit_bytes=8 << 20),
        name="outer",
    )(ids, kept, came_core, came_half)


def precondition_kernel(grads, own, behind, ahead, across_ring, keep, send):
    core, half = core_and_half()
    y = half * 2 + lax.axis_index("grp")
    total = jnp.zeros((128, 256), F32)
    for block, step in ((own, 0), (behind, 1), (ahead, 3), (across_ring, 2)):
        there = (y - step) & 3
        start = pl.multiple_of(((there & 1) * 2 + (there >> 1)) * 512, 512)
        total += lax.dot_general(grads[:, pl.ds(start, 512)], block[...], NT, preferred_element_type=F32)
    low, high = total[:, :128], total[:, 128:]

    @pl.when(core == 0)
    def _():
        keep[...], send[...] = low, high.astype(BF16)

    @pl.when(core != 0)
    def _():
        keep[...], send[...] = high, low.astype(BF16)


def precondition(grads, blocks):
    return pl.pallas_call(
        precondition_kernel,
        out_shape=(jax.ShapeDtypeStruct((128, 128), F32), jax.ShapeDtypeStruct((128, 128), BF16)),
        in_specs=[VMEM] * 5,
        out_specs=(VMEM, VMEM),
        compiler_params=pltpu.CompilerParams(vmem_limit_bytes=8 << 20),
        name="precondition",
    )(grads, *blocks)


def fetch_kernel(store, order, out, sem):
    depth = store.shape[0] // 8
    copies = [
        pltpu.make_async_copy(
            store.at[pl.ds(i * depth, depth), :], out.at[pl.ds(i * depth, depth), :], sem.at[i]
        )
        for i in range(8)
    ]
    for copy in copies:
        copy.start()
    for copy in copies:
        copy.wait()


def fetch(store, order):
    return pl.pallas_call(
        fetch_kernel,
        out_shape=pltpu.VMEM(store.shape, store.dtype),
        in_specs=[HBM, VMEM],
        out_specs=VMEM,
        scratch_shapes=[pltpu.SemaphoreType.DMA((8,))],
        cost_estimate=pl.CostEstimate(flops=0, bytes_accessed=2 * store.size * 2, transcendentals=0),
        compiler_params=pltpu.CompilerParams(vmem_limit_bytes=4 << 20),
        name="fetch",
    )(in_hbm(store), order)


def partial_product(sources, store, blocks, i):
    rows = pl.ds(pl.multiple_of(i * TILE, TILE), TILE)
    core, _ = core_and_half()
    row = lax.axis_index("row")
    total = None
    for (other, step), block in zip(sources, blocks):
        owner = core ^ other
        line = (jnp.where(owner == 0, row >> 2, row & 3) - step) & 3
        stored = []
        for plane in range(4):
            column = jnp.where(owner == 0, 8 * line + 2 * plane, 8 * plane + 2 * line + 1)
            stored.append(store[rows, pl.ds(pl.multiple_of(column * 128, 128), 128)])
        term = lax.dot_general(
            jnp.concatenate(stored, axis=1),
            jnp.concatenate([block[plane] for plane in range(4)], axis=1),
            NT,
            preferred_element_type=F32,
        )
        total = term if total is None else total + term
    return rows, total


def first_kernel(sources, store, *refs):
    *blocks, out = refs

    @pl.loop(0, store.shape[0] // TILE)
    def _(i):
        rows, total = partial_product(sources, store, blocks, i)
        out[rows, :] = total


def next_kernel(sources, store, *refs):
    *blocks, before, out = refs

    @pl.loop(0, store.shape[0] // TILE)
    def _(i):
        rows, total = partial_product(sources, store, blocks, i)
        out[rows, :] = before[rows, :] + total


def last_kernel(sources, store, *refs):
    *blocks, before, order, ids, out, ready, sem = refs

    def leave(i):
        rows = pl.ds(pl.multiple_of(i * TILE, TILE), TILE)
        return pltpu.make_async_copy(ready.at[rows, :], out.at[rows, :], sem.at[i])

    @pl.loop(0, store.shape[0] // TILE)
    def _(i):
        rows, total = partial_product(sources, store, blocks, i)
        total = total + before[rows, :]
        ready[rows, :] = jnp.where(order[rows, :] == ids[...], 0.0, total).astype(BF16)
        leave(i).start()

    @pl.loop(0, store.shape[0] // TILE)
    def _(i):
        leave(i).wait()


def product(kernel, sources, store, blocks, extra, out_shape, out_spec, scratch, name):
    depth = store.shape[0]
    return pl.pallas_call(
        functools.partial(kernel, sources),
        out_shape=out_shape,
        in_specs=[VMEM] * (1 + len(blocks) + len(extra)),
        out_specs=out_spec,
        scratch_shapes=scratch,
        cost_estimate=pl.CostEstimate(
            flops=2 * depth * 512 * 512 * len(blocks), bytes_accessed=depth * 512 * 4, transcendentals=0
        ),
        compiler_params=pltpu.CompilerParams(vmem_limit_bytes=12 << 20),
        name=name,
    )(store, *blocks, *extra)


def local(
    token_ids,
    activations,
    out_grads,
    proj_in,
    proj_out,
    inverse_curvature,
    store_grads,
    store_order,
    example_ids,
):
    width = activations.shape[2]
    flat_inputs = activations.reshape(-1, width)
    flat_grads = out_grads.reshape(-1, width)
    send, keep = project(True, flat_grads, flat_inputs, proj_out, proj_in)
    came = across(send)
    send_kept, kept = project(False, flat_grads, flat_inputs, proj_out, proj_in)
    came_core = across(send_kept)
    passed, curvature = lax.optimization_barrier(
        ((keep + came.astype(F32)).astype(BF16), inverse_curvature)
    )
    came_half = along_y(passed, 2)
    curvature = curvature.astype(BF16)
    blocks = [curvature] + [along_y(curvature, step) for step in STEPS]
    grads = outer(token_ids, kept, came_core, came_half)
    grads = lax.all_to_all(jnp.broadcast_to(grads[None], (16, 8, 16, 128)), "row", 0, 0, tiled=True)
    keep, send = precondition(grads.reshape(128, 2048), blocks)
    mine = (keep + across(send).astype(F32)).astype(BF16)
    own = copied(mine.reshape(16, 8, 128), lambda x, y, z, core: (core, z if core else x))
    own = own.reshape(2, 4, 2, 16, 8, 128).transpose(1, 0, 3, 2, 4, 5).reshape(4, 512, 128)
    own, store_grads, store_order = lax.optimization_barrier((own, store_grads, store_order))
    order, ids = store_order[:, None], example_ids[None, :]
    near = [along_line(own, step) for step in STEPS]
    own_far = across(own)
    store = fetch(store_grads, order)
    depth = store.shape[0]
    part_type = pltpu.VMEM((depth, 512), F32)
    part = product(
        first_kernel, [(0, 0), (1, 0)], store, [own, own_far], [], part_type, VMEM, [], "first"
    )
    near, part = lax.optimization_barrier((near, part))
    far = [across(block) for block in near]
    part = product(
        next_kernel, [(0, step) for step in STEPS], store, near, [part], part_type, VMEM, [], "second"
    )
    return product(
        last_kernel,
        [(1, step) for step in STEPS],
        store,
        far,
        [part, order, ids],
        jax.ShapeDtypeStruct((depth, 512), BF16),
        HBM,
        [pltpu.VMEM((depth, 512), BF16), pltpu.SemaphoreType.DMA((depth // TILE,))],
        "third",
    )


def solution(mesh):
    placed = (
        P(("grp", "row"), None),
        P(("grp", "row"), None, "hid"),
        P(("grp", "row"), None, "hid"),
        P(None, "hid"),
        P(None, "hid"),
        P("row", ("grp", "hid")),
        P(("grp", "row", "hid"), None),
        P(("grp", "row", "hid")),
        P(),
    )
    return jax.shard_map(
        local, mesh=mesh, in_specs=placed, out_specs=P(("grp", "row", "hid"), None), check_vma=False
    )
```

```python
import functools

import jax
import jax.numpy as jnp
from jax import lax
from jax.experimental import pallas as pl
from jax.experimental.pallas import tpu as pltpu
from jax.sharding import PartitionSpec as P


AXES = ("grp", "row", "hid")
NT = (((1,), (1,)), ((), ()))
TN = (((0,), (0,)), ((), ()))
F32 = jnp.float32
BF16 = jnp.bfloat16
VMEM = pl.BlockSpec(memory_space=pltpu.VMEM)
HBM = pl.BlockSpec(memory_space=pltpu.HBM)
TILE = 512
STEPS = (1, 3, 2)


def linear(x, y, z, core):
    return (y % 2) * 64 + (x * 4 + z) * 4 + (y // 2) * 2 + core


def everywhere():
    return [(x, y, z, core) for x in range(4) for y in range(4) for z in range(4) for core in range(2)]


def moved(value, target):
    pairs = [(linear(*place), linear(*target(*place))) for place in everywhere()]
    return lax.ppermute(value, AXES, pairs)


def across(value):
    return moved(value, lambda x, y, z, core: (x, y, z, 1 - core))


def along_y(value, step):
    return moved(value, lambda x, y, z, core: (x, (y + step) % 4, z, core))


def along_line(value, step):
    return moved(
        value,
        lambda x, y, z, core: (x, y, (z + step) % 4, 1) if core else ((x + step) % 4, y, z, 0),
    )


def copied(value, key):
    found = {}
    for place in sorted(everywhere(), key=lambda place: linear(*place)):
        found.setdefault(key(*place), []).append(linear(*place))
    groups = list(found.values())
    count = len(groups[0])
    return lax.all_to_all(
        jnp.broadcast_to(value[None], (count, *value.shape)), AXES, 0, 0, axis_index_groups=groups, tiled=True
    )


def in_hbm(value):
    return pltpu.with_memory_space_constraint(value, pltpu.HBM)


def core_and_half():
    hid = lax.axis_index("hid")
    return hid & 1, hid >> 1


def packed(inside, outside):
    return (
        jnp.concatenate([inside[:256], inside[256:]], axis=1),
        jnp.concatenate([outside[128 * i : 128 * (i + 1)] for i in range(4)], axis=1),
    )


def project_kernel(grads, inputs, w_out, w_in, send, keep, grads_in, inputs_in, out_sorted, in_held, sem, w_sem):
    core, half = core_and_half()
    weights, tiles = [pltpu.make_async_copy(w_in, in_held, w_sem.at[8])], []
    for side in range(2):
        for part in range(4):
            rows = pl.ds(pl.multiple_of((2 * part + (core ^ side)) * 8, 8), 8)
            weights.append(
                pltpu.make_async_copy(
                    w_out.at[rows, :], out_sorted.at[pl.ds(side * 32 + part * 8, 8), :], w_sem.at[side * 4 + part]
                )
            )
    for i in range(4):
        start = (1 - half if i < 2 else half) * 512 + i % 2 * 256
        rows = pl.ds(pl.multiple_of(start, 256), 256)
        tiles.append(pltpu.make_async_copy(inputs.at[rows, :], inputs_in.at[i], sem.at[2 * i]))
        tiles.append(pltpu.make_async_copy(grads.at[rows, :], grads_in.at[i], sem.at[2 * i + 1]))
    for copy in weights + tiles:
        copy.start()
    for copy in weights:
        copy.wait()
    for n in range(2):
        outside, inside = [], []
        for i in (2 * n, 2 * n + 1):
            tiles[2 * i].wait()
            inside.append(lax.dot_general(inputs_in[i], in_held[...], NT, preferred_element_type=F32))
            tiles[2 * i + 1].wait()
            outside.append(lax.dot_general(grads_in[i], out_sorted[...], NT, preferred_element_type=F32))
        outside, inside = jnp.concatenate(outside, axis=0), jnp.concatenate(inside, axis=0)
        ends = ((384 * n, 384 * n + 256), (384 * n + 256, 384 * n + 384))
        for (first, last), value in zip(ends, packed(inside, outside[:, :32])):
            keep[first:last] = value
        for (first, last), value in zip(ends, packed(inside, outside[:, 32:])):
            send[first:last] = value.astype(BF16)


def project(grads, inputs, w_out, w_in):
    tokens, width = grads.shape
    return pl.pallas_call(
        project_kernel,
        out_shape=(jax.ShapeDtypeStruct((768, 128), BF16), jax.ShapeDtypeStruct((768, 128), F32)),
        in_specs=[HBM] * 4,
        out_specs=(VMEM, VMEM),
        scratch_shapes=[
            pltpu.VMEM((4, 256, width), BF16),
            pltpu.VMEM((4, 256, width), BF16),
            pltpu.VMEM((64, width), BF16),
            pltpu.VMEM((64, width), BF16),
            pltpu.SemaphoreType.DMA((8,)),
            pltpu.SemaphoreType.DMA((9,)),
        ],
        cost_estimate=pl.CostEstimate(
            flops=2 * tokens * width * 128, bytes_accessed=2 * tokens * width * 2, transcendentals=0
        ),
        compiler_params=pltpu.CompilerParams(vmem_limit_bytes=12 << 20),
        name="project",
    )(in_hbm(grads), in_hbm(inputs), in_hbm(w_out), in_hbm(w_in))


def outer_kernel(ids, keep, came, came_half, out, held):
    _, half = core_and_half()
    usable = (ids[pl.ds(pl.multiple_of(half * 8, 8), 8), :] > 0).astype(F32)
    counts = jnp.sum(usable, axis=1, keepdims=True)
    total = keep[384:] + came[384:].astype(F32) + came_half[...].astype(F32)
    position = lax.broadcasted_iota(jnp.int32, (64, 32), 0).astype(F32)
    for q in range(8):
        count = counts[q : q + 1]
        inside = total[64 * (q % 4) : 64 * (q % 4 + 1), 64 * (q // 4) : 64 * (q // 4 + 1)]
        outside = total[256 + 64 * (q % 2) : 320 + 64 * (q % 2), 32 * (q // 2) : 32 * (q // 2 + 1)]
        outside = jnp.where(position < count, outside, 0.0)
        held[q] = (
            lax.dot_general(outside.astype(BF16), inside.astype(BF16), TN, preferred_element_type=F32) / count
        )
        even, odd = held[q, pl.ds(0, 16, 2), :], held[q, pl.ds(1, 16, 2), :]
        out[q] = jnp.concatenate([even, odd], axis=1).astype(BF16)


def outer(ids, keep, came, came_half):
    return pl.pallas_call(
        outer_kernel,
        out_shape=jax.ShapeDtypeStruct((8, 16, 128), BF16),
        in_specs=[VMEM] * 4,
        out_specs=VMEM,
        scratch_shapes=[pltpu.VMEM((8, 32, 64), F32)],
        compiler_params=pltpu.CompilerParams(vmem_limit_bytes=8 << 20),
        name="outer",
    )(ids, keep, came, came_half)


def precondition_kernel(grads, own, behind, ahead, across_ring, keep, send):
    core, half = core_and_half()
    y = half * 2 + lax.axis_index("grp")
    total = jnp.zeros((128, 256), F32)
    for block, step in ((own, 0), (behind, 1), (ahead, 3), (across_ring, 2)):
        there = (y - step) & 3
        start = pl.multiple_of(((there & 1) * 2 + (there >> 1)) * 512, 512)
        total += lax.dot_general(grads[:, pl.ds(start, 512)], block[...], NT, preferred_element_type=F32)
    low, high = total[:, :128], total[:, 128:]

    @pl.when(core == 0)
    def _():
        keep[...], send[...] = low, high.astype(BF16)

    @pl.when(core != 0)
    def _():
        keep[...], send[...] = high, low.astype(BF16)


def precondition(grads, blocks):
    return pl.pallas_call(
        precondition_kernel,
        out_shape=(jax.ShapeDtypeStruct((128, 128), F32), jax.ShapeDtypeStruct((128, 128), BF16)),
        in_specs=[VMEM] * 5,
        out_specs=(VMEM, VMEM),
        compiler_params=pltpu.CompilerParams(vmem_limit_bytes=8 << 20),
        name="precondition",
    )(grads, *blocks)


def partial_product(sources, store, blocks, i):
    rows = pl.ds(pl.multiple_of(i * TILE, TILE), TILE)
    core, _ = core_and_half()
    row = lax.axis_index("row")
    total = None
    for (other, step), block in zip(sources, blocks):
        owner = core ^ other
        line = (jnp.where(owner == 0, row >> 2, row & 3) - step) & 3
        stored = []
        for plane in range(4):
            column = jnp.where(owner == 0, 8 * line + 2 * plane, 8 * plane + 2 * line + 1)
            stored.append(store[rows, pl.ds(pl.multiple_of(column * 128, 128), 128)])
        term = lax.dot_general(
            jnp.concatenate(stored, axis=1),
            jnp.concatenate([block[plane] for plane in range(4)], axis=1),
            NT,
            preferred_element_type=F32,
        )
        total = term if total is None else total + term
    return rows, total


def first_kernel(store, own, out, held, sem):
    depth = store.shape[0]
    copies = [
        pltpu.make_async_copy(store.at[pl.ds(i, TILE), :], held.at[pl.ds(i, TILE), :], sem.at[i // TILE])
        for i in range(0, depth, TILE)
    ]
    for copy in copies:
        copy.start()
    for i, copy in enumerate(copies):
        copy.wait()
        out[i * TILE : (i + 1) * TILE, :] = partial_product([(0, 0)], held, [own], i)[1]


def first(store, own):
    depth = store.shape[0]
    return pl.pallas_call(
        first_kernel,
        out_shape=(pltpu.VMEM((depth, 512), F32), pltpu.VMEM(store.shape, store.dtype)),
        in_specs=[HBM, VMEM],
        out_specs=(VMEM, VMEM),
        scratch_shapes=[pltpu.SemaphoreType.DMA((depth // TILE,))],
        cost_estimate=pl.CostEstimate(
            flops=2 * depth * 512 * 512, bytes_accessed=2 * store.size * 2, transcendentals=0
        ),
        compiler_params=pltpu.CompilerParams(vmem_limit_bytes=12 << 20),
        name="first",
    )(in_hbm(store), own)


def next_kernel(sources, store, *refs):
    *blocks, before, out = refs

    @pl.loop(0, store.shape[0] // TILE)
    def _(i):
        rows, total = partial_product(sources, store, blocks, i)
        out[rows, :] = before[rows, :] + total


def last_kernel(sources, store, *refs):
    *blocks, before, order, ids, out, ready, sem = refs

    def leave(i):
        rows = pl.ds(pl.multiple_of(i * TILE, TILE), TILE)
        return pltpu.make_async_copy(ready.at[rows, :], out.at[rows, :], sem.at[i])

    @pl.loop(0, store.shape[0] // TILE)
    def _(i):
        rows, total = partial_product(sources, store, blocks, i)
        total = total + before[rows, :]
        for n in range(TILE // 128):
            column = jnp.broadcast_to(order[pl.ds(i * (TILE // 128) + n, 1), :], (128, 128)).T
            for m in range(4):
                lanes = slice(128 * m, 128 * (m + 1))
                ready[pl.ds(pl.multiple_of(i * TILE + 128 * n, 128), 128), lanes] = jnp.where(
                    column == ids[:, lanes], 0.0, total[128 * n : 128 * (n + 1), lanes]
                ).astype(BF16)
        leave(i).start()

    @pl.loop(0, store.shape[0] // TILE)
    def _(i):
        leave(i).wait()


def product(kernel, sources, store, blocks, extra, out_shape, out_spec, scratch):
    depth = store.shape[0]
    return pl.pallas_call(
        functools.partial(kernel, sources),
        out_shape=out_shape,
        in_specs=[VMEM] * (1 + len(blocks) + len(extra)),
        out_specs=out_spec,
        scratch_shapes=scratch,
        cost_estimate=pl.CostEstimate(
            flops=2 * depth * 512 * 512 * len(blocks), bytes_accessed=depth * 512 * 4, transcendentals=0
        ),
        compiler_params=pltpu.CompilerParams(vmem_limit_bytes=12 << 20),
    )(store, *blocks, *extra)


def local(
    token_ids,
    activations,
    out_grads,
    proj_in,
    proj_out,
    inverse_curvature,
    store_grads,
    store_order,
    example_ids,
):
    width = activations.shape[2]
    flat_inputs = activations.reshape(-1, width)
    flat_grads = out_grads.reshape(-1, width)
    send, keep = project(flat_grads, flat_inputs, proj_out, proj_in)
    came = across(send)
    passed = (keep[:384] + came[:384].astype(F32)).astype(BF16)
    came_half = along_y(passed, 2)
    curvature = inverse_curvature.astype(BF16)
    blocks = [curvature] + [along_y(curvature, step) for step in STEPS]
    grads = outer(token_ids, keep, came, came_half)
    grads = lax.all_to_all(jnp.broadcast_to(grads[None], (16, 8, 16, 128)), "row", 0, 0, tiled=True)
    keep, send = precondition(grads.reshape(128, 2048), blocks)
    mine = (keep + across(send).astype(F32)).astype(BF16)
    own = copied(mine.reshape(16, 8, 128), lambda x, y, z, core: (core, z if core else x))
    own = own.reshape(2, 4, 2, 16, 8, 128).transpose(1, 0, 3, 2, 4, 5).reshape(4, 512, 128)
    near = {}
    for step in STEPS:
        near[step] = along_line(own, step)
    own_far = across(own)
    part, store = first(store_grads, own)
    depth = store.shape[0]

    def added(kernel, sources, blocks, before):
        out = pltpu.VMEM((depth, 512), F32)
        return product(kernel, sources, store, blocks, before, out, VMEM, [])

    near[1], near[3], part = lax.optimization_barrier((near[1], near[3], part))
    far = dict((step, across(near[step])) for step in (1, 3))
    part = added(next_kernel, [(1, 0), (0, 1), (0, 3)], [own_far, near[1], near[3]], [part])
    part = added(next_kernel, [(1, 1), (1, 3)], [far[1], far[3]], [part])
    near[2], part = lax.optimization_barrier((near[2], part))
    far[2] = across(near[2])
    part = added(next_kernel, [(0, 2)], [near[2]], [part])
    return product(
        last_kernel,
        [(1, 2)],
        store,
        [far[2]],
        [part, store_order.reshape(depth // 128, 128), example_ids[None, :]],
        jax.ShapeDtypeStruct((depth, 512), BF16),
        HBM,
        [pltpu.VMEM((depth, 512), BF16), pltpu.SemaphoreType.DMA((depth // TILE,))],
    )


def solution(mesh):
    placed = (
        P(("grp", "row"), None),
        P(("grp", "row"), None, "hid"),
        P(("grp", "row"), None, "hid"),
        P(None, "hid"),
        P(None, "hid"),
        P("row", ("grp", "hid")),
        P(("grp", "row", "hid"), None),
        P(("grp", "row", "hid")),
        P(),
    )

    return jax.shard_map(local, mesh=mesh, in_specs=placed, out_specs=P(("grp", "row", "hid"), None), check_vma=False)
```

```python
import functools

import jax
import jax.numpy as jnp
from jax import lax
from jax.experimental import pallas as pl
from jax.experimental.pallas import tpu as pltpu
from jax.sharding import PartitionSpec as P


AXES = ("grp", "row", "hid")
NT = (((1,), (1,)), ((), ()))
TN = (((0,), (0,)), ((), ()))
F32 = jnp.float32
BF16 = jnp.bfloat16
VMEM = pl.BlockSpec(memory_space=pltpu.VMEM)
HBM = pl.BlockSpec(memory_space=pltpu.HBM)
TILE = 512
STEPS = (1, 3, 2)
ALL, LOW, HIGH = range(4), range(2), range(2, 4)


def linear(x, y, z, core):
    return (y % 2) * 64 + (x * 4 + z) * 4 + (y // 2) * 2 + core


def everywhere():
    return [(x, y, z, core) for x in range(4) for y in range(4) for z in range(4) for core in range(2)]


def moved(value, target):
    pairs = [(linear(*place), linear(*target(*place))) for place in everywhere()]
    return lax.ppermute(value, AXES, pairs)


def across(value):
    return moved(value, lambda x, y, z, core: (x, y, z, 1 - core))


def along_y(value, step):
    return moved(value, lambda x, y, z, core: (x, (y + step) % 4, z, core))


def along_line(value, step):
    return moved(
        value,
        lambda x, y, z, core: (x, y, (z + step) % 4, 1) if core else ((x + step) % 4, y, z, 0),
    )


def copied(value, key):
    found = {}
    for place in sorted(everywhere(), key=lambda place: linear(*place)):
        found.setdefault(key(*place), []).append(linear(*place))
    groups = list(found.values())
    count = len(groups[0])
    return lax.all_to_all(
        jnp.broadcast_to(value[None], (count, *value.shape)), AXES, 0, 0, axis_index_groups=groups, tiled=True
    )


def in_hbm(value):
    return pltpu.with_memory_space_constraint(value, pltpu.HBM)


def core_and_half():
    hid = lax.axis_index("hid")
    return hid & 1, hid >> 1


def packed(inside, outside):
    return (
        jnp.concatenate([inside[:256], inside[256:]], axis=1),
        jnp.concatenate([outside[128 * i : 128 * (i + 1)] for i in range(4)], axis=1),
    )


def project_kernel(grads, inputs, w_out, w_in, send, keep, grads_in, inputs_in, out_sorted, in_held, sem, w_sem):
    core, half = core_and_half()
    weights, tiles = [pltpu.make_async_copy(w_in, in_held, w_sem.at[8])], []
    for side in range(2):
        for part in range(4):
            rows = pl.ds(pl.multiple_of((2 * part + (core ^ side)) * 8, 8), 8)
            weights.append(
                pltpu.make_async_copy(
                    w_out.at[rows, :], out_sorted.at[pl.ds(side * 32 + part * 8, 8), :], w_sem.at[side * 4 + part]
                )
            )
    for n in range(2):
        rows = pl.ds(pl.multiple_of((half if n else 1 - half) * 512, 512), 512)
        tiles.append(pltpu.make_async_copy(inputs.at[rows, :], inputs_in.at[n], sem.at[2 * n]))
        tiles.append(pltpu.make_async_copy(grads.at[rows, :], grads_in.at[n], sem.at[2 * n + 1]))
    for copy in weights + tiles:
        copy.start()
    for copy in weights:
        copy.wait()
    for n in range(2):
        tiles[2 * n].wait()
        inside = lax.dot_general(inputs_in[n], in_held[...], NT, preferred_element_type=F32)
        tiles[2 * n + 1].wait()
        outside = lax.dot_general(grads_in[n], out_sorted[...], NT, preferred_element_type=F32)
        ends = ((384 * n, 384 * n + 256), (384 * n + 256, 384 * n + 384))
        for (first, last), value in zip(ends, packed(inside, outside[:, :32])):
            keep[first:last] = value
        for (first, last), value in zip(ends, packed(inside, outside[:, 32:])):
            send[first:last] = value.astype(BF16)


def project(grads, inputs, w_out, w_in):
    tokens, width = grads.shape
    return pl.pallas_call(
        project_kernel,
        out_shape=(jax.ShapeDtypeStruct((768, 128), BF16), jax.ShapeDtypeStruct((768, 128), F32)),
        in_specs=[HBM] * 4,
        out_specs=(VMEM, VMEM),
        scratch_shapes=[
            pltpu.VMEM((2, 512, width), BF16),
            pltpu.VMEM((2, 512, width), BF16),
            pltpu.VMEM((64, width), BF16),
            pltpu.VMEM((64, width), BF16),
            pltpu.SemaphoreType.DMA((4,)),
            pltpu.SemaphoreType.DMA((9,)),
        ],
        cost_estimate=pl.CostEstimate(
            flops=2 * tokens * width * 128, bytes_accessed=2 * tokens * width * 2, transcendentals=0
        ),
        compiler_params=pltpu.CompilerParams(vmem_limit_bytes=12 << 20),
        name="project",
    )(in_hbm(grads), in_hbm(inputs), in_hbm(w_out), in_hbm(w_in))


def outer_kernel(ids, keep, came, came_half, out, held):
    _, half = core_and_half()
    usable = (ids[pl.ds(pl.multiple_of(half * 8, 8), 8), :] > 0).astype(F32)
    counts = jnp.sum(usable, axis=1, keepdims=True)
    total = keep[384:] + came[384:].astype(F32) + came_half[...].astype(F32)
    position = lax.broadcasted_iota(jnp.int32, (64, 32), 0).astype(F32)
    for q in range(8):
        count = counts[q : q + 1]
        inside = total[64 * (q % 4) : 64 * (q % 4 + 1), 64 * (q // 4) : 64 * (q // 4 + 1)]
        outside = total[256 + 64 * (q % 2) : 320 + 64 * (q % 2), 32 * (q // 2) : 32 * (q // 2 + 1)]
        outside = jnp.where(position < count, outside, 0.0)
        held[q] = (
            lax.dot_general(outside.astype(BF16), inside.astype(BF16), TN, preferred_element_type=F32) / count
        )
        even, odd = held[q, pl.ds(0, 16, 2), :], held[q, pl.ds(1, 16, 2), :]
        out[q] = jnp.concatenate([even, odd], axis=1).astype(BF16)


def outer(ids, keep, came, came_half):
    return pl.pallas_call(
        outer_kernel,
        out_shape=jax.ShapeDtypeStruct((8, 16, 128), BF16),
        in_specs=[VMEM] * 4,
        out_specs=VMEM,
        scratch_shapes=[pltpu.VMEM((8, 32, 64), F32)],
        compiler_params=pltpu.CompilerParams(vmem_limit_bytes=8 << 20),
        name="outer",
    )(ids, keep, came, came_half)


def precondition_kernel(grads, own, behind, ahead, across_ring, keep, send):
    core, half = core_and_half()
    y = half * 2 + lax.axis_index("grp")
    total = jnp.zeros((128, 256), F32)
    for block, step in ((own, 0), (behind, 1), (ahead, 3), (across_ring, 2)):
        there = (y - step) & 3
        start = pl.multiple_of(((there & 1) * 2 + (there >> 1)) * 512, 512)
        total += lax.dot_general(grads[:, pl.ds(start, 512)], block[...], NT, preferred_element_type=F32)
    low, high = total[:, :128], total[:, 128:]

    @pl.when(core == 0)
    def _():
        keep[...], send[...] = low, high.astype(BF16)

    @pl.when(core != 0)
    def _():
        keep[...], send[...] = high, low.astype(BF16)


def precondition(grads, blocks):
    return pl.pallas_call(
        precondition_kernel,
        out_shape=(jax.ShapeDtypeStruct((128, 128), F32), jax.ShapeDtypeStruct((128, 128), BF16)),
        in_specs=[VMEM] * 5,
        out_specs=(VMEM, VMEM),
        compiler_params=pltpu.CompilerParams(vmem_limit_bytes=8 << 20),
        name="precondition",
    )(grads, *blocks)


def partial_product(sources, store, blocks, i):
    rows = pl.ds(pl.multiple_of(i * TILE, TILE), TILE)
    core, _ = core_and_half()
    row = lax.axis_index("row")
    total = None
    for (other, step, planes), block in zip(sources, blocks):
        owner = core ^ other
        line = (jnp.where(owner == 0, row >> 2, row & 3) - step) & 3
        stored = []
        for plane in planes:
            column = jnp.where(owner == 0, 8 * line + 2 * plane, 8 * plane + 2 * line + 1)
            stored.append(store[rows, pl.ds(pl.multiple_of(column * 128, 128), 128)])
        term = lax.dot_general(
            jnp.concatenate(stored, axis=1),
            jnp.concatenate([block[n] for n in range(len(planes))], axis=1),
            NT,
            preferred_element_type=F32,
        )
        total = term if total is None else total + term
    return rows, total


def first_kernel(store, own, out, held, sem):
    depth = store.shape[0]
    copies = [
        pltpu.make_async_copy(store.at[pl.ds(i, TILE), :], held.at[pl.ds(i, TILE), :], sem.at[i // TILE])
        for i in range(0, depth, TILE)
    ]
    for copy in copies:
        copy.start()
    for i, copy in enumerate(copies):
        copy.wait()
        out[i * TILE : (i + 1) * TILE, :] = partial_product([(0, 0, ALL)], held, [own], i)[1]


def first(store, own):
    depth = store.shape[0]
    return pl.pallas_call(
        first_kernel,
        out_shape=(pltpu.VMEM((depth, 512), F32), pltpu.VMEM(store.shape, store.dtype)),
        in_specs=[HBM, VMEM],
        out_specs=(VMEM, VMEM),
        scratch_shapes=[pltpu.SemaphoreType.DMA((depth // TILE,))],
        cost_estimate=pl.CostEstimate(
            flops=2 * depth * 512 * 512, bytes_accessed=2 * store.size * 2, transcendentals=0
        ),
        compiler_params=pltpu.CompilerParams(vmem_limit_bytes=12 << 20),
        name="first",
    )(in_hbm(store), own)


def next_kernel(sources, store, *refs):
    *blocks, before, out = refs

    @pl.loop(0, store.shape[0] // TILE)
    def _(i):
        rows, total = partial_product(sources, store, blocks, i)
        out[rows, :] = before[rows, :] + total


def last_kernel(sources, store, *refs):
    *blocks, before, order, ids, out, ready, sem = refs

    def leave(i):
        rows = pl.ds(pl.multiple_of(i * TILE, TILE), TILE)
        return pltpu.make_async_copy(ready.at[rows, :], out.at[rows, :], sem.at[i])

    @pl.loop(0, store.shape[0] // TILE)
    def _(i):
        rows, total = partial_product(sources, store, blocks, i)
        total = total + before[rows, :]
        for n in range(TILE // 128):
            column = jnp.broadcast_to(order[pl.ds(i * (TILE // 128) + n, 1), :], (128, 128)).T
            for m in range(4):
                lanes = slice(128 * m, 128 * (m + 1))
                ready[pl.ds(pl.multiple_of(i * TILE + 128 * n, 128), 128), lanes] = jnp.where(
                    column == ids[:, lanes], 0.0, total[128 * n : 128 * (n + 1), lanes]
                ).astype(BF16)
        leave(i).start()

    @pl.loop(0, store.shape[0] // TILE)
    def _(i):
        leave(i).wait()


def product(kernel, sources, store, blocks, extra, out_shape, out_spec, scratch):
    depth = store.shape[0]
    return pl.pallas_call(
        functools.partial(kernel, sources),
        out_shape=out_shape,
        in_specs=[VMEM] * (1 + len(blocks) + len(extra)),
        out_specs=out_spec,
        scratch_shapes=scratch,
        cost_estimate=pl.CostEstimate(
            flops=2 * depth * 512 * 128 * sum(len(source[2]) for source in sources), bytes_accessed=depth * 512 * 4, transcendentals=0
        ),
        compiler_params=pltpu.CompilerParams(vmem_limit_bytes=12 << 20),
    )(store, *blocks, *extra)


def local(
    token_ids,
    activations,
    out_grads,
    proj_in,
    proj_out,
    inverse_curvature,
    store_grads,
    store_order,
    example_ids,
):
    width = activations.shape[2]
    flat_inputs = activations.reshape(-1, width)
    flat_grads = out_grads.reshape(-1, width)
    send, keep = project(flat_grads, flat_inputs, proj_out, proj_in)
    came = across(send)
    passed = (keep[:384] + came[:384].astype(F32)).astype(BF16)
    came_half = along_y(passed, 2)
    curvature = inverse_curvature.astype(BF16)
    blocks = [curvature] + [along_y(curvature, step) for step in STEPS]
    grads = outer(token_ids, keep, came, came_half)
    grads = lax.all_to_all(jnp.broadcast_to(grads[None], (16, 8, 16, 128)), "row", 0, 0, tiled=True)
    keep, send = precondition(grads.reshape(128, 2048), blocks)
    mine = (keep + across(send).astype(F32)).astype(BF16)
    own = copied(mine.reshape(16, 8, 128), lambda x, y, z, core: (core, z if core else x))
    own = own.reshape(2, 4, 2, 16, 8, 128).transpose(1, 0, 3, 2, 4, 5).reshape(4, 512, 128)
    near = {}
    for step in (1, 3):
        near[step] = along_line(own, step)
    own_far = across(own)
    part, store = first(store_grads, own)
    depth = store.shape[0]

    def added(kernel, sources, blocks, before):
        out = pltpu.VMEM((depth, 512), F32)
        return product(kernel, sources, store, blocks, before, out, VMEM, [])

    near[1], near[3], part = lax.optimization_barrier((near[1], near[3], part))
    passed_1 = along_line(near[1][:2], 1)
    passed_3 = along_line(near[3][2:], 3)
    far = dict((step, across(near[step])) for step in (1, 3))
    part = added(next_kernel, [(1, 0, ALL), (0, 1, ALL), (0, 3, ALL)], [own_far, near[1], near[3]], [part])
    passed_1, passed_3, part = lax.optimization_barrier((passed_1, passed_3, part))
    far_1, far_3 = across(passed_1), across(passed_3)
    part = added(next_kernel, [(1, 1, ALL), (1, 3, ALL)], [far[1], far[3]], [part])
    return product(
        last_kernel,
        [(0, 2, LOW), (0, 2, HIGH), (1, 2, LOW), (1, 2, HIGH)],
        store,
        [passed_1, passed_3, far_1, far_3],
        [part, store_order.reshape(depth // 128, 128), example_ids[None, :]],
        jax.ShapeDtypeStruct((depth, 512), BF16),
        HBM,
        [pltpu.VMEM((depth, 512), BF16), pltpu.SemaphoreType.DMA((depth // TILE,))],
    )


def solution(mesh):
    placed = (
        P(("grp", "row"), None),
        P(("grp", "row"), None, "hid"),
        P(("grp", "row"), None, "hid"),
        P(None, "hid"),
        P(None, "hid"),
        P("row", ("grp", "hid")),
        P(("grp", "row", "hid"), None),
        P(("grp", "row", "hid")),
        P(),
    )

    return jax.shard_map(local, mesh=mesh, in_specs=placed, out_specs=P(("grp", "row", "hid"), None), check_vma=False)
```
